512 devices in a mesh: row: 32 (over y, x), col: 16 (over z, core).
Axes of the slice: x: 4, y: 8, z: 8, core: 2. Of those that a mesh axis runs over, the one named last changes fastest.
Arguments:
- density: bfloat16 [4096, 4096], P('row', 'col'), as said below
- cotangent: bfloat16 [4096, 4096], P('row', 'col'), may hold values from -6 to 6
- block_pattern: int32 [64, 64], P('row', 'col'), may hold values from 0 to 1, as said below
- filter_pattern: int32 [64, 64], P('row', 'col'), may hold values from 0 to 1, as said below
Outputs:
- purified: bfloat16 [4096, 4096], P('row', 'col')
- gradient: bfloat16 [4096, 4096], P('row', 'col')
The draws below stay inside these ranges and needn't reach their ends.
Inputs may be any that keep to these rules, and one draw needn't show every extreme that they name: density is symmetric. `block_pattern`: symmetric, with ones on the diagonal. `filter_pattern`: symmetric, with ones on the diagonal.
All inputs are finite; a program needn't handle non-finite values.
Results may differ from the reference program's by a relative error of at most 0.0043.
Values may be sent and summed in bfloat16 or wider, within the bound.
A program may use at most 64 MiB of HBM per device.

```python
import jax
import jax.numpy as jnp

BS = 64
N = 4096


def draw_density(key, part):
    raw = jax.random.normal(key, (N, N), jnp.float32)
    symmetric = (raw + raw.T) * 0.7071
    return (symmetric * (0.5 * N ** (-0.25))).astype(jnp.bfloat16)


def pattern_from(key, offset):
    block_count = N // BS
    upper = jax.random.randint(key, (block_count, block_count), 0, 100)
    row_index = jnp.arange(block_count)[:, None]
    col_index = jnp.arange(block_count)[None, :]
    symmetric = jnp.where(row_index <= col_index, upper, upper.T)
    threshold = 15 + offset + 60 * (row_index + col_index) // (2 * block_count - 1)
    chosen = (symmetric < threshold) | (row_index == col_index)
    return jnp.where(chosen, 1, 0).astype(jnp.int32)


def draw_block_pattern(key, part):
    return pattern_from(jax.random.fold_in(key, 11), 0)


def draw_filter_pattern(key, part):
    return pattern_from(jax.random.fold_in(key, 23), 20)


def levels(own_key, dims, shards, least, high):
    def one(axis_at, parts):
        heights = jax.random.uniform(jax.random.fold_in(jax.random.fold_in(own_key, 6), axis_at), (parts,), jnp.float32, least / len(shards), high / len(shards))
        return jnp.repeat(jnp.exp(heights), dims[axis_at] // parts).reshape((-1,) + (1,) * (len(dims) - axis_at - 1))

    gain = one(*shards[0])
    for cut in shards[1:]:
        gain = gain * one(*cut)
    return gain


def bell_draw(rng, extent, deviation, most, split=(), held_as=jnp.bfloat16):
    drawn = jax.random.normal(rng, extent, jnp.float32) * deviation
    if len(split) > 0:
        drawn = levels(rng, extent, split, -0.22, 0.18) * drawn
    return jnp.clip(drawn, min=-most, max=most).astype(held_as)


def setup_inputs(seed: int = 0) -> dict:
    key_list = jax.random.split(jax.random.key(seed), 5)
    density = draw_density(jax.random.fold_in(key_list[4], 71), 0)
    cotangent = bell_draw(key_list[1], (N, N), 1.0, 6.0, ((0, 32), (1, 16)))
    block_pattern = draw_block_pattern(jax.random.fold_in(key_list[4], 71), 0)
    filter_pattern = draw_filter_pattern(jax.random.fold_in(key_list[4], 71), 0)
    return {"density": density, "cotangent": cotangent, "block_pattern": block_pattern, "filter_pattern": filter_pattern}


def expand(pattern, block_size):
    spread = jnp.repeat(jnp.repeat(pattern, block_size, axis=0), block_size, axis=1)
    return spread.astype(jnp.float32)


def reference(density, cotangent, block_pattern, filter_pattern):
    keep_p = expand(block_pattern, BS)
    keep_f = expand(filter_pattern, BS)
    masked = (density.astype(jnp.float32) * keep_p).astype(jnp.bfloat16)
    square = (jnp.dot(masked, masked, preferred_element_type=jnp.float32) * keep_f).astype(jnp.bfloat16)
    cubic_term = jnp.dot(square, masked, preferred_element_type=jnp.float32) * keep_f
    purified = (3.0 * square.astype(jnp.float32) - 2.0 * cubic_term).astype(jnp.bfloat16)
    weighted = (-2.0 * cotangent.astype(jnp.float32) * keep_f).astype(jnp.bfloat16)
    back_term = jnp.dot(weighted, masked, preferred_element_type=jnp.float32)
    square_grad = ((3.0 * cotangent.astype(jnp.float32) + back_term) * keep_f).astype(jnp.bfloat16)
    summed = jnp.dot(square, weighted, preferred_element_type=jnp.float32)
    summed = summed + jnp.dot(square_grad, masked, preferred_element_type=jnp.float32)
    summed = summed + jnp.dot(masked, square_grad, preferred_element_type=jnp.float32)
    gradient = (summed * keep_p).astype(jnp.bfloat16)
    return purified, gradient
```

```python
import functools

import jax
import jax.numpy as jnp
from jax import lax
from jax.experimental import pallas as pl
from jax.experimental.pallas import tpu as pltpu
from jax.sharding import PartitionSpec as P

MESH = pl.DeviceIdType.MESH
X = 4
MID_TYPE = jnp.float32
END_TYPE = jnp.bfloat16
N_SEM = 224


class Net:
    def __init__(self, send_sem, recv_sem):
        self.send_sem, self.recv_sem, self.used, self.sent = send_sem, recv_sem, 0, []

    def take(self, count):
        first = self.used
        self.used += count
        assert self.used <= N_SEM
        return first

    def send(self, src, dst, sem, recv, device):
        copy = pltpu.make_async_remote_copy(
            src_ref=src,
            dst_ref=dst,
            send_sem=self.send_sem.at[sem],
            recv_sem=self.recv_sem.at[recv],
            device_id=device,
            device_id_type=MESH,
        )
        copy.start()
        self.sent.append((copy, None))

    def send_or_keep(self, src, dst, sem, recv, device, is_self):
        copy = pltpu.make_async_remote_copy(
            src_ref=src,
            dst_ref=dst,
            send_sem=self.send_sem.at[sem],
            recv_sem=self.recv_sem.at[recv],
            device_id=device,
            device_id_type=MESH,
        )

        @pl.when(is_self)
        def _():
            pltpu.make_async_copy(src, dst, self.recv_sem.at[recv]).start()

        @pl.when(jnp.logical_not(is_self))
        def _():
            copy.start()

        self.sent.append((copy, is_self))

    def wait(self, dst, recv):
        pltpu.make_async_copy(dst, dst, self.recv_sem.at[recv]).wait()

    def drain(self):
        for copy, is_self in self.sent:
            if is_self is None:
                copy.wait_send()
            else:

                @pl.when(jnp.logical_not(is_self))
                def _():
                    copy.wait_send()


class Ring:
    def __init__(self, net, view, me, n, plus, minus, partner=None, other=None, long_plus=True):
        self.net, self.view, self.me, self.n = net, view, me, n
        self.plus, self.minus, self.partner, self.other = plus, minus, partner, other
        half, rest = n // 2, n - 1 - n // 2
        self.hops = (half, rest) if long_plus else (rest, half)
        self.up, self.down = net.take(self.hops[0]), net.take(self.hops[1])
        if partner is not None:
            self.cross = net.take(n)

    def block(self, hop, sign):
        return lax.rem(self.me + self.n - sign * hop, self.n)

    def start(self):
        mine = self.view(self.me)
        if self.hops[0]:
            self.net.send(mine, mine, self.up, self.up, self.plus)
        if self.hops[1]:
            self.net.send(mine, mine, self.down, self.down, self.minus)
        if self.partner is not None:
            self.net.send(mine, mine, self.cross, self.cross, self.partner)

    def step(self, s):
        for way, sign, first, to in ((0, 1, self.up, self.plus), (1, -1, self.down, self.minus)):
            if s < self.hops[way]:
                got = self.view(self.block(s + 1, sign))
                self.net.wait(got, first + s)
                if s + 1 < self.hops[way]:
                    self.net.send(got, got, first + s + 1, first + s + 1, to)
                if self.partner is not None:
                    at = self.cross + 1 + s + way * self.hops[0]
                    self.net.send(got, got, at, at, self.partner)

    def steps(self):
        return max(self.hops)

    def finish_cross(self):
        self.net.wait(self.other(self.me), self.cross)
        for way, sign in ((0, 1), (1, -1)):
            for s in range(self.hops[way]):
                at = self.cross + 1 + s + way * self.hops[0]
                self.net.wait(self.other(self.block(s + 1, sign)), at)


def spread(pattern, rows):
    lane = lax.broadcasted_iota(jnp.int32, (rows // 2, 256), 1)
    halves = []
    for i in range(2):
        e = [pattern[i, j].astype(jnp.float32) for j in range(4)]
        low = jnp.where(lane < 64, e[0], e[1])
        high = jnp.where(lane < 192, e[2], e[3])
        halves.append(jnp.where(lane < 128, low, high))
    return jnp.concatenate(halves, axis=0)


def kernel(
    ny, nz, den_ref, cot_ref, pat_ref, fil_ref, pur_ref, grad_ref,
    am, aw, asq, ag, bm, bw, bg, keep_mine, keep_tile, part_s, part_g, got_s, got_g, square_end,
    end_p, end_g, got_p, got_d, send_sem, recv_sem,
):
    row, col = lax.axis_index("row"), lax.axis_index("col")
    x, y = lax.rem(row, X), lax.div(row, X)
    core, z = lax.rem(col, 2), lax.div(col, 2)

    def dev(yy, xx, zz, cc):
        return (yy * X + xx, zz * 2 + cc)

    partner = dev(y, x, z, 1 - core)
    y_up, y_down = dev(lax.rem(y + 1, ny), x, z, core), dev(lax.rem(y + ny - 1, ny), x, z, core)
    z_up, z_down = dev(y, x, lax.rem(z + 1, nz), core), dev(y, x, lax.rem(z + nz - 1, nz), core)
    others = [partner, y_up, y_down, z_up, z_down]
    for d in range(1, X):
        there = lax.rem(x + d, X)
        others += [dev(y, there, z, core), dev(y, there, z, 1 - core)]

    barrier = pltpu.get_barrier_semaphore()
    for other in others:
        pl.semaphore_signal(barrier, inc=1, device_id=other, device_id_type=MESH)
    keep_p = spread(pat_ref, 128)
    keep_f = spread(fil_ref, 128)
    bm[y, core] = (den_ref[...].astype(jnp.float32) * keep_p).astype(jnp.bfloat16)
    bw[y, core] = (-2.0 * cot_ref[...].astype(jnp.float32) * keep_f).astype(jnp.bfloat16)
    keep_mine[...] = keep_f.astype(jnp.bfloat16)
    pl.semaphore_wait(barrier, len(others))

    net = Net(send_sem, recv_sem)
    slot = lax.rem(x, 2)
    home = lax.div(x, 2)

    def swap(src, dst):
        send, recv = net.take(2), net.take(2)
        for j in range(2):
            is_self = jnp.logical_and(x == 2 * core + j, home == core)
            net.send_or_keep(src(j), dst(slot), send + j, recv + slot, dev(y, 2 * core + j, z, home), is_self)
        return recv

    def to_rows(own, tile):
        return (lambda j: own.at[:, pl.ds(128 * j, 128)]), (lambda s: tile.at[pl.ds(pl.multiple_of(128 * s, 128), 128), :])

    def to_cols(tile, own):
        return (lambda j: tile.at[pl.ds(128 * j, 128), :]), (lambda s: own.at[:, pl.ds(pl.multiple_of(128 * s, 128), 128)])

    def wait_swap(dst, recv):
        for s in range(2):
            net.wait(dst(s), recv + s)

    def b_ring(buf, long_plus):
        return Ring(net, lambda k: buf.at[k, core], y, ny, y_up, y_down, partner, lambda k: buf.at[k, 1 - core], long_plus)

    def a_ring(buf, long_plus):
        return Ring(net, lambda k: buf.at[k], z, nz, z_up, z_down, None, None, long_plus)

    def product(a, b, h):
        left = jnp.concatenate([a[k] for k in range(nz)], axis=1)
        right = b[:, h].reshape(ny * 128, 256)
        return jnp.dot(left, right, preferred_element_type=jnp.float32)

    def part(a, b, to):
        for h in range(2):
            value = product(a, b, h)
            to[2 * h] = value[:, :128]
            to[2 * h + 1] = value[:, 128:]

    def reduce_start(src, dst):
        sems = net.take(X)
        for d in range(1, X):
            there = lax.rem(x + d, X)
            net.send(src.at[there], dst.at[d], sems + d, sems + d, dev(y, there, z, core))
        return sems

    def reduce_end(src, dst, sems):
        total = src[x]
        for d in range(1, X):
            net.wait(dst.at[d], sems + d)
            total = total + dst[d].astype(jnp.float32)
        return total

    def end_start(src, dst):
        send, recv = net.take(4), net.take(X)
        for j in range(2):
            for h in range(2):
                is_self = jnp.logical_and(x == 2 * core + j, core == h)
                net.send_or_keep(src.at[j, h], dst.at[x], send + 2 * j + h, recv + x, dev(y, 2 * core + j, z, h), is_self)
        return recv

    def end_sum(dst, recv):
        total = None
        for s in range(X):
            net.wait(dst.at[s], recv + s)
            term = dst[s].astype(jnp.float32)
            total = term if total is None else total + term
        return total

    w_src, w_dst = to_rows(bw.at[y, core], aw.at[z])
    m_src, m_dst = to_rows(bm.at[y, core], am.at[z])
    f_src, f_dst = to_rows(keep_mine, keep_tile)
    w_swap = swap(w_src, w_dst)
    m_swap = swap(m_src, m_dst)
    ring_bm = b_ring(bm, True)
    ring_bm.start()
    f_swap = swap(f_src, f_dst)
    ring_aw, ring_am = a_ring(aw, True), a_ring(am, False)
    wait_swap(w_dst, w_swap)
    ring_aw.start()
    wait_swap(m_dst, m_swap)
    ring_am.start()
    for s in range(ring_bm.steps()):
        ring_bm.step(s)
        ring_aw.step(s)
        ring_am.step(s)
    ring_bm.finish_cross()

    part(aw, bm, part_g)
    g_sems = reduce_start(part_g, got_g)
    part(am, bm, part_s)
    s_sems = reduce_start(part_s, got_s)
    ring_bw = b_ring(bw, False)
    ring_bw.start()
    wait_swap(f_dst, f_swap)

    grad = -1.5 * aw[z].astype(jnp.float32) + reduce_end(part_g, got_g, g_sems)
    ag[z] = (grad * keep_tile[...].astype(jnp.float32)).astype(jnp.bfloat16)
    ring_ag = a_ring(ag, True)
    ring_ag.start()
    g_src, g_dst = to_cols(ag.at[z], bg.at[y, core])
    g_swap = swap(g_src, lambda s: bg.at[y, home, :, pl.ds(pl.multiple_of(128 * s, 128), 128)])

    asq[z] = (reduce_end(part_s, got_s, s_sems) * keep_tile[...].astype(jnp.float32)).astype(jnp.bfloat16)
    ring_as = a_ring(asq, False)
    ring_as.start()
    wait_swap(g_dst, g_swap)
    ring_bg = b_ring(bg, True)
    ring_bg.start()
    q_src, q_dst = to_cols(asq.at[z], square_end)
    q_swap = swap(q_src, q_dst)
    for s in range(ring_bw.steps()):
        ring_bw.step(s)
        ring_ag.step(s)
        ring_as.step(s)
        ring_bg.step(s)
    ring_bw.finish_cross()

    for h in range(2):
        value = product(asq, bm, h).astype(END_TYPE)
        for j in range(2):
            end_p[j, h] = value[128 * j : 128 * j + 128]
    p_recv = end_start(end_p, got_p)
    ring_bg.finish_cross()
    for h in range(2):
        value = (product(asq, bw, h) + product(ag, bm, h) + product(am, bg, h)).astype(END_TYPE)
        for j in range(2):
            end_g[j, h] = value[128 * j : 128 * j + 128]
    d_recv = end_start(end_g, got_d)

    wait_swap(q_dst, q_swap)
    cubic = end_sum(got_p, p_recv) * keep_mine[...].astype(jnp.float32)
    pur_ref[...] = (3.0 * square_end[...].astype(jnp.float32) - 2.0 * cubic).astype(jnp.bfloat16)
    grad_ref[...] = (end_sum(got_d, d_recv) * spread(pat_ref, 128)).astype(jnp.bfloat16)
    net.drain()


def on_device(ny, nz, density, cotangent, block_pattern, filter_pattern):
    bf16, f32 = jnp.bfloat16, jnp.float32
    left = pltpu.VMEM((nz, 256, 128), bf16)
    right = pltpu.VMEM((ny, 2, 128, 256), bf16)
    block = pltpu.VMEM((128, 256), bf16)
    vmem = pl.BlockSpec(memory_space=pltpu.VMEM)
    smem = pl.BlockSpec(memory_space=pltpu.SMEM)
    return pl.pallas_call(
        functools.partial(kernel, ny, nz),
        out_shape=(jax.ShapeDtypeStruct((128, 256), bf16),) * 2,
        in_specs=[vmem, vmem, smem, smem],
        out_specs=(vmem, vmem),
        scratch_shapes=[left] * 4
        + [right] * 3
        + [
            block,
            pltpu.VMEM((256, 128), bf16),
            pltpu.VMEM((X, 256, 128), f32),
            pltpu.VMEM((X, 256, 128), f32),
            pltpu.VMEM((X, 256, 128), MID_TYPE),
            pltpu.VMEM((X, 256, 128), MID_TYPE),
            block,
            pltpu.VMEM((2, 2, 128, 256), END_TYPE),
            pltpu.VMEM((2, 2, 128, 256), END_TYPE),
            pltpu.VMEM((X, 128, 256), END_TYPE),
            pltpu.VMEM((X, 128, 256), END_TYPE),
            pltpu.SemaphoreType.DMA((N_SEM,)),
            pltpu.SemaphoreType.DMA((N_SEM,)),
        ],
        compiler_params=pltpu.CompilerParams(collective_id=0, has_side_effects=True),
    )(density, cotangent, block_pattern, filter_pattern)


def solution(mesh):
    ny, nz = mesh.shape["row"] // X, mesh.shape["col"] // 2
    placed = (P("row", "col"),) * 4
    return jax.shard_map(
        functools.partial(on_device, ny, nz),
        mesh=mesh,
        in_specs=placed,
        out_specs=(P("row", "col"), P("row", "col")),
        check_vma=False,
    )
```

```python
import functools

import jax
import jax.numpy as jnp
from jax import lax
from jax.experimental import pallas as pl
from jax.experimental.pallas import tpu as pltpu
from jax.sharding import PartitionSpec as P

MESH = pl.DeviceIdType.MESH
X = 4
MID_TYPE = jnp.bfloat16
END_TYPE = jnp.bfloat16
N_SEM = 100
PLAN = dict(bm="two", aw="two", am="two", bw="two", ag="two", asq="two", bg="two")
PLANS = {
    "ring": (((0, None, 1), (0, None, -1)), ((-1, None, 1), (1, None, -1)), ((-2, None, 1), (2, None, -1)), ((-3, 0, 1), (3, 1, -1))),
    "two": (((0, None, 2), (0, None, -2), (0, None, 1), (0, None, -1)), ((-2, None, 1), (2, None, -1), (-2, 0, 2), (2, 1, -2))),
}
FAR = 2


class Net:
    def __init__(self, sems, ruler, at_home):
        self.sems, self.ruler, self.at_home, self.used, self.later = sems, ruler, at_home, 0, []

    def take(self):
        self.used += 1
        assert self.used <= N_SEM
        return self.used - 1

    def copy(self, src, dst, send, recv, device):
        return pltpu.make_async_remote_copy(
            src_ref=src,
            dst_ref=dst,
            send_sem=self.sems.at[send],
            recv_sem=self.sems.at[recv],
            device_id=device,
            device_id_type=MESH,
        )

    def send(self, src, dst, send, recv, device):
        self.copy(src, dst, send, recv, device).start()

    def send_or_keep(self, src, dst, send, recv, device, is_self):
        @pl.when(is_self)
        def _():
            pltpu.make_async_copy(src, dst, self.sems.at[recv]).start()

        @pl.when(jnp.logical_not(is_self))
        def _():
            self.copy(src, dst, send, recv, device).start()

    def wait(self, dst, sem):
        pltpu.make_async_copy(dst, dst, self.sems.at[sem]).wait()

    def sent(self, sem, units, home_units=None):
        self.later.append((sem, units, home_units))

    def wait_units(self, sem, units):
        view = self.ruler.at[0, pl.ds(0, 128)] if units == 1 else self.ruler.at[pl.ds(0, units // 2)]
        self.wait(view, sem)

    def drain(self):
        for sem, units, home_units in self.later:
            if home_units is None:
                self.wait_units(sem, units)
            else:
                pl.when(self.at_home)(functools.partial(self.wait_units, sem, home_units))
                pl.when(jnp.logical_not(self.at_home))(functools.partial(self.wait_units, sem, units))


class Gather:
    def __init__(self, net, view, me, n, device, plan, pieces=None, partner=None, other=None):
        self.net, self.view, self.me, self.n, self.device = net, view, me, n, device
        self.pieces, self.partner, self.other = pieces, partner, other
        self.stages = PLANS[plan] if n == 8 else (tuple((0, None, o) for o in range(1, n)),)
        self.recv, self.halves = {}, {}
        if pieces is not None:
            self.recv[0], self.home_sem = net.take(), net.take()
            net.sent(self.home_sem, 2, 1)
        self.sem, units = net.take(), 0
        for stage in self.stages:
            for want, half, o in stage:
                relative = (want - o) % n
                if relative not in self.recv:
                    self.recv[relative] = net.take()
                units += 2 if half is None else 1
        net.sent(self.sem, units)
        self.here = set() if pieces is not None else {0}
        if partner is not None:
            self.cross_send, self.cross_recv = net.take(), net.take()
            net.sent(self.cross_send, 2 * n)

    def block(self, relative):
        return lax.rem(self.me + relative + 2 * self.n, self.n)

    def cross(self, relative):
        if self.partner is not None:
            got = self.view(self.block(relative), None)
            self.net.send(got, got, self.cross_send, self.cross_recv, self.partner)

    def arrive(self, relative):
        relative %= self.n
        if relative not in self.here:
            self.here.add(relative)
            self.net.wait(self.view(self.block(relative), None), self.recv[relative])
            return relative
        return None

    def start(self):
        if self.pieces is not None:
            self.pieces(0, self.home_sem, self.recv[0])
        self.stage(0)
        if self.pieces is None:
            self.cross(0)

    def stage(self, i):
        for want, half, o in self.stages[i]:
            if self.pieces is not None and want == 0:
                self.pieces(o, self.sem, self.recv[-o % self.n])
                continue
            new = self.arrive(want)
            got = self.view(self.block(want), half)
            self.net.send(got, got, self.sem, self.recv[(want - o) % self.n], self.device(o))
            if new is not None:
                self.cross(new)

    def finish(self):
        for relative in self.recv:
            new = self.arrive(relative)
            if new is not None:
                self.cross(new)

    def finish_cross(self):
        self.net.wait(self.other, self.cross_recv)


def interleave(*gathers):
    for i in range(1, max(len(g.stages) for g in gathers)):
        for g in gathers:
            if i < len(g.stages):
                g.stage(i)


def spread(pattern, rows):
    lane = lax.broadcasted_iota(jnp.int32, (rows // 2, 256), 1)
    halves = []
    for i in range(2):
        e = [pattern[i, j].astype(jnp.float32) for j in range(4)]
        low = jnp.where(lane < 64, e[0], e[1])
        high = jnp.where(lane < 192, e[2], e[3])
        halves.append(jnp.where(lane < 128, low, high))
    return jnp.concatenate(halves, axis=0)


def kernel(
    ny, nz, den_ref, cot_ref, pat_ref, fil_ref, pur_ref, grad_ref,
    am, aw, asq, ag, bm, bw, bg, keep_mine, keep_tile, part_s, part_g, wire_s, wire_g, got_s, got_g, square_end,
    total, end_p, end_g, got_p, got_d, sems,
):
    row, col = lax.axis_index("row"), lax.axis_index("col")
    x, y = lax.rem(row, X), lax.div(row, X)
    core, z = lax.rem(col, 2), lax.div(col, 2)
    slot, home = lax.rem(x, 2), lax.div(x, 2)

    def dev(yy, xx, zz, cc):
        return (yy * X + xx, zz * 2 + cc)

    def along_y(o, xx, cc):
        return dev(lax.rem(y + o + ny, ny), xx, z, cc)

    def along_z(o, xx, cc):
        return dev(y, xx, lax.rem(z + o + nz, nz), cc)

    def at_y(o):
        return along_y(o, x, core)

    def at_z(o):
        return along_z(o, x, core)

    partner = dev(y, x, z, 1 - core)
    others = [partner]
    for d in range(1, X):
        there = lax.rem(x + d, X)
        others += [dev(y, there, z, core), dev(y, there, z, 1 - core)]
    for n, along in ((ny, along_y), (nz, along_z)):
        for o in [o for a in range(1, FAR + 1) for o in (a, -a)] if n == 8 else range(1, n):
            others += [along(o, x, core), along(o, 2 * core, home), along(o, 2 * core + 1, home)]

    barrier = pltpu.get_barrier_semaphore()
    for other in others:
        pl.semaphore_signal(barrier, inc=1, device_id=other, device_id_type=MESH)
    keep_p = spread(pat_ref, 128)
    keep_f = spread(fil_ref, 128)
    bm[y, core] = (den_ref[...].astype(jnp.float32) * keep_p).astype(jnp.bfloat16)
    bw[y, core] = (-2.0 * cot_ref[...].astype(jnp.float32) * keep_f).astype(jnp.bfloat16)
    keep_mine[...] = keep_f.astype(jnp.bfloat16)
    pl.semaphore_wait(barrier, len(others))

    net = Net(sems, am, home == core)

    def swap_pieces(src, dst, along):
        def pieces(o, send, recv):
            for j in range(2):
                there = along(o, 2 * core + j, home)
                if o == 0:
                    is_self = jnp.logical_and(x == 2 * core + j, home == core)
                    net.send_or_keep(src(j), dst(slot), send, recv, there, is_self)
                else:
                    net.send(src(j), dst(slot), send, recv, there)

        return pieces

    def swap(src, dst):
        send, recv = net.take(), net.take()
        swap_pieces(src, dst, along_z)(0, send, recv)
        net.sent(send, 2, 1)
        return recv

    def to_rows(own, tile):
        return (lambda j: own.at[:, pl.ds(128 * j, 128)]), (lambda s: tile.at[pl.ds(pl.multiple_of(128 * s, 128), 128), :])

    def to_cols(tile, own):
        return (lambda j: tile.at[pl.ds(128 * j, 128), :]), (lambda s: own.at[:, pl.ds(pl.multiple_of(128 * s, 128), 128)])

    def rows_half(ref, half, size):
        return ref if half is None else ref.at[pl.ds(half * size, size), :]

    def b_gather(buf, plan, pieces=None):
        return Gather(
            net, lambda k, h: rows_half(buf.at[k, core], h, 64), y, ny, at_y, plan, pieces, partner, buf.at[:, 1 - core]
        )

    def a_gather(buf, plan, pieces=None):
        return Gather(net, lambda k, h: rows_half(buf.at[k], h, 128), z, nz, at_z, plan, pieces)

    def product(a, b, h):
        left = jnp.concatenate([a[k] for k in range(nz)], axis=1)
        right = b[:, h].reshape(ny * 128, 256)
        return jnp.dot(left, right, preferred_element_type=jnp.float32)

    def part(a, b, to, wire):
        for h in range(2):
            value = product(a, b, h)
            for i in range(2):
                to[2 * h + i] = value[:, 128 * i : 128 * i + 128]
                wire[2 * h + i] = value[:, 128 * i : 128 * i + 128].astype(MID_TYPE)

    def reduce_start(src, dst):
        send, recv = net.take(), net.take()
        for d in (2, 1, 3):
            there = lax.rem(x + d, X)
            net.send(src.at[there], dst.at[d], send, recv, dev(y, there, z, core))
        net.sent(send, 6 if MID_TYPE == jnp.bfloat16 else 12)
        return recv

    def reduce_end(src, dst, recv):
        net.wait(dst.at[pl.ds(1, X - 1)], recv)
        total = src[x]
        for d in range(1, X):
            total = total + dst[d].astype(jnp.float32)
        return total

    def end_start(src, dst):
        send, recv = net.take(), net.take()
        for j in range(2):
            for h in range(2):
                is_self = jnp.logical_and(x == 2 * core + j, core == h)
                net.send_or_keep(src.at[j, h], dst.at[x], send, recv, dev(y, 2 * core + j, z, h), is_self)
        scale = 1 if END_TYPE == jnp.bfloat16 else 2
        net.sent(send, 8 * scale, 6 * scale)
        return recv

    def end_sum(dst, recv):
        net.wait(dst, recv)
        value = dst[0].astype(jnp.float32)
        for s in range(1, X):
            value = value + dst[s].astype(jnp.float32)
        return value

    def split(value, h, to):
        for j in range(2):
            to[j, h] = value[128 * j : 128 * j + 128].astype(END_TYPE)

    w_src, w_dst = to_rows(bw.at[y, core], aw.at[z])
    m_src, m_dst = to_rows(bm.at[y, core], am.at[z])
    f_src, f_dst = to_rows(keep_mine, keep_tile)
    all_aw = a_gather(aw, PLAN["aw"], swap_pieces(w_src, w_dst, along_z))
    all_am = a_gather(am, PLAN["am"], swap_pieces(m_src, m_dst, along_z))
    all_bm = b_gather(bm, PLAN["bm"])
    all_aw.start()
    all_bm.start()
    all_am.start()
    f_recv = swap(f_src, f_dst)
    interleave(all_aw, all_bm, all_am)
    all_bm.finish()
    all_aw.finish()
    all_bm.finish_cross()

    part(aw, bm, part_g, wire_g)
    g_recv = reduce_start(wire_g, got_g)
    all_am.finish()
    part(am, bm, part_s, wire_s)
    s_recv = reduce_start(wire_s, got_s)
    all_bw = b_gather(bw, PLAN["bw"])
    all_bw.start()
    net.wait(keep_tile, f_recv)

    grad = -1.5 * aw[z].astype(jnp.float32) + reduce_end(part_g, got_g, g_recv)
    ag[z] = (grad * keep_tile[...].astype(jnp.float32)).astype(jnp.bfloat16)
    all_ag = a_gather(ag, PLAN["ag"])
    g_src = to_cols(ag.at[z], None)[0]
    g_dst = lambda s: bg.at[y, home, :, pl.ds(pl.multiple_of(128 * s, 128), 128)]
    g_pieces = swap_pieces(g_src, g_dst, along_y)
    all_bg = b_gather(bg, PLAN["bg"], g_pieces)
    all_bg.start()
    all_ag.start()

    asq[z] = (reduce_end(part_s, got_s, s_recv) * keep_tile[...].astype(jnp.float32)).astype(jnp.bfloat16)
    all_as = a_gather(asq, PLAN["asq"])
    all_as.start()
    q_src, q_dst = to_cols(asq.at[z], square_end)
    q_recv = swap(q_src, q_dst)
    interleave(all_bg, all_ag, all_as, all_bw)
    all_bw.finish()
    all_bg.finish()
    all_bw.finish_cross()
    all_as.finish()

    for h in range(2):
        split(product(asq, bm, h), h, end_p)
    p_recv = end_start(end_p, got_p)
    for h in range(2):
        total[h] = product(asq, bw, h)
    all_ag.finish()
    for h in range(2):
        total[h] += product(ag, bm, h)
    all_bg.finish_cross()
    for h in range(2):
        split(total[h] + product(am, bg, h), h, end_g)
    d_recv = end_start(end_g, got_d)

    net.wait(square_end, q_recv)
    cubic = end_sum(got_p, p_recv) * keep_mine[...].astype(jnp.float32)
    pur_ref[...] = (3.0 * square_end[...].astype(jnp.float32) - 2.0 * cubic).astype(jnp.bfloat16)
    grad_ref[...] = (end_sum(got_d, d_recv) * spread(pat_ref, 128)).astype(jnp.bfloat16)
    net.drain()


def on_device(ny, nz, density, cotangent, block_pattern, filter_pattern):
    bf16, f32 = jnp.bfloat16, jnp.float32
    left = pltpu.VMEM((nz, 256, 128), bf16)
    right = pltpu.VMEM((ny, 2, 128, 256), bf16)
    block = pltpu.VMEM((128, 256), bf16)
    vmem = pl.BlockSpec(memory_space=pltpu.VMEM)
    smem = pl.BlockSpec(memory_space=pltpu.SMEM)
    return pl.pallas_call(
        functools.partial(kernel, ny, nz),
        out_shape=(jax.ShapeDtypeStruct((128, 256), bf16),) * 2,
        in_specs=[vmem, vmem, smem, smem],
        out_specs=(vmem, vmem),
        scratch_shapes=[left] * 4
        + [right] * 3
        + [
            block,
            pltpu.VMEM((256, 128), bf16),
            pltpu.VMEM((X, 256, 128), f32),
            pltpu.VMEM((X, 256, 128), f32),
            pltpu.VMEM((X, 256, 128), MID_TYPE),
            pltpu.VMEM((X, 256, 128), MID_TYPE),
            pltpu.VMEM((X, 256, 128), MID_TYPE),
            pltpu.VMEM((X, 256, 128), MID_TYPE),
            block,
            pltpu.VMEM((2, 256, 256), f32),
            pltpu.VMEM((2, 2, 128, 256), END_TYPE),
            pltpu.VMEM((2, 2, 128, 256), END_TYPE),
            pltpu.VMEM((X, 128, 256), END_TYPE),
            pltpu.VMEM((X, 128, 256), END_TYPE),
            pltpu.SemaphoreType.DMA((N_SEM,)),
        ],
        compiler_params=pltpu.CompilerParams(collective_id=0, has_side_effects=True),
    )(density, cotangent, block_pattern, filter_pattern)


def solution(mesh):
    ny, nz = mesh.shape["row"] // X, mesh.shape["col"] // 2
    placed = (P("row", "col"),) * 4
    return jax.shard_map(
        functools.partial(on_device, ny, nz),
        mesh=mesh,
        in_specs=placed,
        out_specs=(P("row", "col"), P("row", "col")),
        check_vma=False,
    )
```

```python
import functools

import jax
import jax.numpy as jnp
from jax import lax
from jax.experimental import pallas as pl
from jax.experimental.pallas import tpu as pltpu
from jax.sharding import PartitionSpec as P

MESH = pl.DeviceIdType.MESH
X = 4
MID_TYPE = jnp.bfloat16
END_TYPE = jnp.bfloat16
N_SEM = 80
PLAN = dict(bm="two", aw="far", am="far", bw="two", ag="two", asq="two", bg="far")
PLANS = {
    "two": (((0, None, 2), (0, None, -2), (0, None, 1), (0, None, -1)), ((-2, 0, 2), (2, 1, -2), (-2, None, 1), (2, None, -1))),
    "far": (((0, None, 2), (0, None, -2)), ((0, None, 1), (0, None, -1), (-2, 0, 2), (2, 1, -2), (-2, None, 1), (2, None, -1))),
}
OFFSETS = (1, -1, 2, -2)


class Net:
    def __init__(self, sems, ruler, at_home):
        self.sems, self.ruler, self.at_home, self.used, self.later = sems, ruler, at_home, 0, []

    def take(self):
        self.used += 1
        assert self.used <= N_SEM
        return self.used - 1

    def copy(self, src, dst, send, recv, device):
        return pltpu.make_async_remote_copy(
            src_ref=src,
            dst_ref=dst,
            send_sem=self.sems.at[send],
            recv_sem=self.sems.at[recv],
            device_id=device,
            device_id_type=MESH,
        )

    def send(self, src, dst, send, recv, device):
        self.copy(src, dst, send, recv, device).start()

    def send_or_keep(self, src, dst, send, recv, device, is_self):
        @pl.when(is_self)
        def _():
            pltpu.make_async_copy(src, dst, self.sems.at[recv]).start()

        @pl.when(jnp.logical_not(is_self))
        def _():
            self.copy(src, dst, send, recv, device).start()

    def wait(self, dst, sem):
        pltpu.make_async_copy(dst, dst, self.sems.at[sem]).wait()

    def sent(self, sem, units, home_units=None):
        self.later.append((sem, units, home_units))

    def wait_units(self, sem, units):
        view = self.ruler.at[0, pl.ds(0, 128)] if units == 1 else self.ruler.at[pl.ds(0, units // 2)]
        self.wait(view, sem)

    def drain(self):
        for sem, units, home_units in self.later:
            if home_units is None:
                self.wait_units(sem, units)
            else:
                pl.when(self.at_home)(functools.partial(self.wait_units, sem, home_units))
                pl.when(jnp.logical_not(self.at_home))(functools.partial(self.wait_units, sem, units))


class Gather:
    def __init__(self, net, view, me, n, device, plan, pieces=None, partner=None, other=None):
        self.net, self.view, self.me, self.n, self.device = net, view, me, n, device
        self.pieces, self.partner, self.other = pieces, partner, other
        self.stages = PLANS[plan] if n == 8 else (tuple((0, None, o) for o in range(1, n)),)
        self.recv, self.halves = {}, {}
        if pieces is not None:
            self.recv[0], self.home_sem = net.take(), net.take()
            net.sent(self.home_sem, 2, 1)
        self.sem, units = net.take(), 0
        for stage in self.stages:
            for want, half, o in stage:
                relative = (want - o) % n
                if relative not in self.recv:
                    self.recv[relative] = net.take()
                units += 2 if half is None else 1
        net.sent(self.sem, units)
        self.here = set() if pieces is not None else {0}
        if partner is not None:
            self.cross_send, self.cross_recv = net.take(), net.take()
            net.sent(self.cross_send, 2 * n)

    def block(self, relative):
        return lax.rem(self.me + relative + 2 * self.n, self.n)

    def cross(self, relative):
        if self.partner is not None:
            got = self.view(self.block(relative), None)
            self.net.send(got, got, self.cross_send, self.cross_recv, self.partner)

    def arrive(self, relative):
        relative %= self.n
        if relative not in self.here:
            self.here.add(relative)
            self.net.wait(self.view(self.block(relative), None), self.recv[relative])
            return relative
        return None

    def start(self):
        if self.pieces is not None:
            self.pieces(0, self.home_sem, self.recv[0])
        self.stage(0)
        if self.pieces is None:
            self.cross(0)

    def stage(self, i):
        for want, half, o in self.stages[i]:
            if self.pieces is not None and want == 0 and i == 0:
                self.pieces(o, self.sem, self.recv[-o % self.n])
                continue
            new = self.arrive(want)
            got = self.view(self.block(want), half)
            self.net.send(got, got, self.sem, self.recv[(want - o) % self.n], self.device(o))
            if new is not None:
                self.cross(new)

    def finish(self):
        for relative in self.recv:
            new = self.arrive(relative)
            if new is not None:
                self.cross(new)

    def finish_cross(self):
        self.net.wait(self.other, self.cross_recv)


def interleave(*gathers):
    for i in range(1, max(len(g.stages) for g in gathers)):
        for g in gathers:
            if i < len(g.stages):
                g.stage(i)


def spread(pattern, rows):
    lane = lax.broadcasted_iota(jnp.int32, (rows // 2, 256), 1)
    halves = []
    for i in range(2):
        e = [pattern[i, j].astype(jnp.float32) for j in range(4)]
        low = jnp.where(lane < 64, e[0], e[1])
        high = jnp.where(lane < 192, e[2], e[3])
        halves.append(jnp.where(lane < 128, low, high))
    return jnp.concatenate(halves, axis=0)


def kernel(
    ny, nz, den_hbm, cot_hbm, pat_hbm, fil_hbm, pur_ref, grad_ref, den_ref, cot_ref, pat_ref, fil_ref,
    am, aw, asq, ag, bm, bw, bg, keep_mine, keep_tile, part_s, part_g, wire_s, wire_g, got_s, got_g, square_end,
    total, end_p, end_g, got_p, got_d, sems,
):
    row, col = lax.axis_index("row"), lax.axis_index("col")
    x, y = lax.rem(row, X), lax.div(row, X)
    core, z = lax.rem(col, 2), lax.div(col, 2)
    slot, home = lax.rem(x, 2), lax.div(x, 2)

    def dev(yy, xx, zz, cc):
        return (yy * X + xx, zz * 2 + cc)

    def along_y(o, xx, cc):
        return dev(lax.rem(y + o + ny, ny), xx, z, cc)

    def along_z(o, xx, cc):
        return dev(y, xx, lax.rem(z + o + nz, nz), cc)

    def at_y(o):
        return along_y(o, x, core)

    def at_z(o):
        return along_z(o, x, core)

    partner = dev(y, x, z, 1 - core)
    others = [partner]
    for d in range(1, X):
        there = lax.rem(x + d, X)
        others += [dev(y, there, z, core), dev(y, there, z, 1 - core)]
    for n, along in ((ny, along_y), (nz, along_z)):
        for o in OFFSETS if n == 8 else range(1, n):
            others += [along(o, x, core)]
            if abs(o) == 2 or n != 8:
                others += [along(o, 2 * core, home), along(o, 2 * core + 1, home)]

    barrier = pltpu.get_barrier_semaphore()
    for other in others:
        pl.semaphore_signal(barrier, inc=1, device_id=other, device_id_type=MESH)
    loads = ((den_hbm, den_ref), (cot_hbm, cot_ref), (pat_hbm, pat_ref), (fil_hbm, fil_ref))
    loads = [pltpu.make_async_copy(src, dst, sems.at[N_SEM + i]) for i, (src, dst) in enumerate(loads)]
    for load in loads:
        load.start()
    for load in loads:
        load.wait()
    keep_p = spread(pat_ref, 128)
    keep_f = spread(fil_ref, 128)
    bm[y, core] = (den_ref[...].astype(jnp.float32) * keep_p).astype(jnp.bfloat16)
    bw[y, core] = (-2.0 * cot_ref[...].astype(jnp.float32) * keep_f).astype(jnp.bfloat16)
    keep_mine[...] = keep_f.astype(jnp.bfloat16)
    pl.semaphore_wait(barrier, len(others))

    net = Net(sems, am, home == core)

    def swap_pieces(src, dst, along):
        def pieces(o, send, recv):
            for j in range(2):
                there = along(o, 2 * core + j, home)
                if o == 0:
                    is_self = jnp.logical_and(x == 2 * core + j, home == core)
                    net.send_or_keep(src(j), dst(slot), send, recv, there, is_self)
                else:
                    net.send(src(j), dst(slot), send, recv, there)

        return pieces

    def swap(src, dst):
        send, recv = net.take(), net.take()
        swap_pieces(src, dst, along_z)(0, send, recv)
        net.sent(send, 2, 1)
        return recv

    def to_rows(own, tile):
        return (lambda j: own.at[:, pl.ds(128 * j, 128)]), (lambda s: tile.at[pl.ds(pl.multiple_of(128 * s, 128), 128), :])

    def to_cols(tile, own):
        return (lambda j: tile.at[pl.ds(128 * j, 128), :]), (lambda s: own.at[:, pl.ds(pl.multiple_of(128 * s, 128), 128)])

    def rows_half(ref, half, size):
        return ref if half is None else ref.at[pl.ds(half * size, size), :]

    def b_gather(buf, plan, pieces=None):
        return Gather(
            net, lambda k, h: rows_half(buf.at[k, core], h, 64), y, ny, at_y, plan, pieces, partner, buf.at[:, 1 - core]
        )

    def a_gather(buf, plan, pieces=None):
        return Gather(net, lambda k, h: rows_half(buf.at[k], h, 128), z, nz, at_z, plan, pieces)

    def product(a, b, h):
        left = jnp.concatenate([a[k] for k in range(nz)], axis=1)
        right = b[:, h].reshape(ny * 128, 256)
        return jnp.dot(left, right, preferred_element_type=jnp.float32)

    def part(a, b, to, wire):
        for h in range(2):
            value = product(a, b, h)
            for i in range(2):
                to[2 * h + i] = value[:, 128 * i : 128 * i + 128]
                wire[2 * h + i] = value[:, 128 * i : 128 * i + 128].astype(MID_TYPE)

    def reduce_start(src, dst):
        send, recv = net.take(), net.take()
        for d in (2, 1, 3):
            there = lax.rem(x + d, X)
            net.send(src.at[there], dst.at[d], send, recv, dev(y, there, z, core))
        net.sent(send, 6 if MID_TYPE == jnp.bfloat16 else 12)
        return recv

    def reduce_end(src, dst, recv):
        net.wait(dst.at[pl.ds(1, X - 1)], recv)
        total = src[x]
        for d in range(1, X):
            total = total + dst[d].astype(jnp.float32)
        return total

    def end_start(src, dst):
        send, recv = net.take(), net.take()
        for j in range(2):
            for h in range(2):
                is_self = jnp.logical_and(x == 2 * core + j, core == h)
                net.send_or_keep(src.at[j, h], dst.at[x], send, recv, dev(y, 2 * core + j, z, h), is_self)
        scale = 1 if END_TYPE == jnp.bfloat16 else 2
        net.sent(send, 8 * scale, 6 * scale)
        return recv

    def end_sum(dst, recv):
        net.wait(dst, recv)
        value = dst[0].astype(jnp.float32)
        for s in range(1, X):
            value = value + dst[s].astype(jnp.float32)
        return value

    def split(value, h, to):
        for j in range(2):
            to[j, h] = value[128 * j : 128 * j + 128].astype(END_TYPE)

    w_src, w_dst = to_rows(bw.at[y, core], aw.at[z])
    m_src, m_dst = to_rows(bm.at[y, core], am.at[z])
    f_src, f_dst = to_rows(keep_mine, keep_tile)
    all_bm = b_gather(bm, PLAN["bm"])
    all_bw = b_gather(bw, PLAN["bw"])
    all_aw = a_gather(aw, PLAN["aw"], swap_pieces(w_src, w_dst, along_z))
    all_am = a_gather(am, PLAN["am"], swap_pieces(m_src, m_dst, along_z))
    all_aw.start()
    all_bm.start()
    all_am.start()
    f_recv = swap(f_src, f_dst)
    interleave(all_bm, all_aw, all_am)
    all_bm.finish()
    all_aw.finish()
    all_bm.finish_cross()

    part(aw, bm, part_g, wire_g)
    g_recv = reduce_start(wire_g, got_g)
    all_am.finish()
    part(am, bm, part_s, wire_s)
    s_recv = reduce_start(wire_s, got_s)
    all_bw.start()
    net.wait(keep_tile, f_recv)

    grad = -1.5 * aw[z].astype(jnp.float32) + reduce_end(part_g, got_g, g_recv)
    ag[z] = (grad * keep_tile[...].astype(jnp.float32)).astype(jnp.bfloat16)
    all_ag = a_gather(ag, PLAN["ag"])
    g_src = to_cols(ag.at[z], None)[0]
    g_dst = lambda s: bg.at[y, home, :, pl.ds(pl.multiple_of(128 * s, 128), 128)]
    g_pieces = swap_pieces(g_src, g_dst, along_y)
    all_bg = b_gather(bg, PLAN["bg"], g_pieces)
    all_bg.start()
    all_ag.start()

    asq[z] = (reduce_end(part_s, got_s, s_recv) * keep_tile[...].astype(jnp.float32)).astype(jnp.bfloat16)
    all_as = a_gather(asq, PLAN["asq"])
    all_as.start()
    q_src, q_dst = to_cols(asq.at[z], square_end)
    q_recv = swap(q_src, q_dst)
    interleave(all_ag, all_bg, all_as, all_bw)
    all_bw.finish()
    all_as.finish()
    all_bw.finish_cross()

    for h in range(2):
        split(product(asq, bm, h), h, end_p)
    p_recv = end_start(end_p, got_p)
    for h in range(2):
        total[h] = product(asq, bw, h)
    all_ag.finish()
    for h in range(2):
        total[h] += product(ag, bm, h)
    all_bg.finish()
    split(total[core] + product(am, bg, core), core, end_g)
    all_bg.finish_cross()
    split(total[1 - core] + product(am, bg, 1 - core), 1 - core, end_g)
    d_recv = end_start(end_g, got_d)

    net.wait(square_end, q_recv)
    cubic = end_sum(got_p, p_recv) * keep_mine[...].astype(jnp.float32)
    pur_ref[...] = (3.0 * square_end[...].astype(jnp.float32) - 2.0 * cubic).astype(jnp.bfloat16)
    grad_ref[...] = (end_sum(got_d, d_recv) * spread(pat_ref, 128)).astype(jnp.bfloat16)
    net.drain()


def on_device(ny, nz, density, cotangent, block_pattern, filter_pattern):
    bf16, f32 = jnp.bfloat16, jnp.float32
    left = pltpu.VMEM((nz, 256, 128), bf16)
    right = pltpu.VMEM((ny, 2, 128, 256), bf16)
    block = pltpu.VMEM((128, 256), bf16)
    vmem = pl.BlockSpec(memory_space=pltpu.VMEM)
    return pl.pallas_call(
        functools.partial(kernel, ny, nz),
        out_shape=(jax.ShapeDtypeStruct((128, 256), bf16),) * 2,
        in_specs=[pl.BlockSpec(memory_space=pl.ANY)] * 4,
        out_specs=(vmem, vmem),
        scratch_shapes=[block] * 2
        + [pltpu.SMEM((2, 4), jnp.int32)] * 2
        + [left] * 4
        + [right] * 3
        + [
            block,
            pltpu.VMEM((256, 128), bf16),
            pltpu.VMEM((X, 256, 128), f32),
            pltpu.VMEM((X, 256, 128), f32),
            pltpu.VMEM((X, 256, 128), MID_TYPE),
            pltpu.VMEM((X, 256, 128), MID_TYPE),
            pltpu.VMEM((X, 256, 128), MID_TYPE),
            pltpu.VMEM((X, 256, 128), MID_TYPE),
            block,
            pltpu.VMEM((2, 256, 256), f32),
            pltpu.VMEM((2, 2, 128, 256), END_TYPE),
            pltpu.VMEM((2, 2, 128, 256), END_TYPE),
            pltpu.VMEM((X, 128, 256), END_TYPE),
            pltpu.VMEM((X, 128, 256), END_TYPE),
            pltpu.SemaphoreType.DMA((N_SEM + 4,)),
        ],
        compiler_params=pltpu.CompilerParams(collective_id=0, has_side_effects=True),
    )(density, cotangent, block_pattern, filter_pattern)


def solution(mesh):
    ny, nz = mesh.shape["row"] // X, mesh.shape["col"] // 2
    placed = (P("row", "col"),) * 4
    return jax.shard_map(
        functools.partial(on_device, ny, nz),
        mesh=mesh,
        in_specs=placed,
        out_specs=(P("row", "col"), P("row", "col")),
        check_vma=False,
    )
```

```python
import functools

import jax
import jax.numpy as jnp
from jax import lax
from jax.experimental import pallas as pl
from jax.experimental.pallas import tpu as pltpu
from jax.sharding import PartitionSpec as P

MESH = pl.DeviceIdType.MESH
X = 4
MID_TYPE = jnp.bfloat16
END_TYPE = jnp.bfloat16
N_SEM = 80
PLAN = dict(bm="two", aw="far", am="far", bw="two", ag="two", asq="two", bg="far")
PLANS = {
    "two": (((0, None, 2), (0, None, -2), (0, None, 1), (0, None, -1)), ((-2, 0, 2), (2, 1, -2), (-2, None, 1), (2, None, -1))),
    "far": (((0, None, 2), (0, None, -2)), ((0, None, 1), (0, None, -1), (-2, 0, 2), (2, 1, -2), (-2, None, 1), (2, None, -1))),
}
OFFSETS = (1, -1, 2, -2)


class Net:
    def __init__(self, sems, ruler, at_home):
        self.sems, self.ruler, self.at_home, self.used, self.later = sems, ruler, at_home, 0, []

    def take(self):
        self.used += 1
        assert self.used <= N_SEM
        return self.used - 1

    def copy(self, src, dst, send, recv, device):
        return pltpu.make_async_remote_copy(
            src_ref=src,
            dst_ref=dst,
            send_sem=self.sems.at[send],
            recv_sem=self.sems.at[recv],
            device_id=device,
            device_id_type=MESH,
        )

    def send(self, src, dst, send, recv, device):
        self.copy(src, dst, send, recv, device).start()

    def send_or_keep(self, src, dst, send, recv, device, is_self):
        @pl.when(is_self)
        def _():
            pltpu.make_async_copy(src, dst, self.sems.at[recv]).start()

        @pl.when(jnp.logical_not(is_self))
        def _():
            self.copy(src, dst, send, recv, device).start()

    def wait(self, dst, sem):
        pltpu.make_async_copy(dst, dst, self.sems.at[sem]).wait()

    def sent(self, sem, units, home_units=None):
        self.later.append((sem, units, home_units))

    def wait_units(self, sem, units):
        view = self.ruler.at[0, pl.ds(0, 128)] if units == 1 else self.ruler.at[pl.ds(0, units // 2)]
        self.wait(view, sem)

    def drain(self):
        for sem, units, home_units in self.later:
            if home_units is None:
                self.wait_units(sem, units)
            else:
                pl.when(self.at_home)(functools.partial(self.wait_units, sem, home_units))
                pl.when(jnp.logical_not(self.at_home))(functools.partial(self.wait_units, sem, units))


class Gather:
    def __init__(self, net, view, me, n, device, plan, pieces=None, partner=None, other=None):
        self.net, self.view, self.me, self.n, self.device = net, view, me, n, device
        self.pieces, self.partner, self.other = pieces, partner, other
        self.stages = PLANS[plan] if n == 8 else (tuple((0, None, o) for o in range(1, n)),)
        self.recv, self.halves = {}, {}
        if pieces is not None:
            self.recv[0], self.home_sem = net.take(), net.take()
            net.sent(self.home_sem, 2, 1)
        self.sem, units = net.take(), 0
        for stage in self.stages:
            for want, half, o in stage:
                relative = (want - o) % n
                if relative not in self.recv:
                    self.recv[relative] = net.take()
                units += 2 if half is None else 1
        net.sent(self.sem, units)
        self.here = set() if pieces is not None else {0}
        if partner is not None:
            self.cross_send, self.cross_recv = net.take(), net.take()
            net.sent(self.cross_send, 2 * n)

    def block(self, relative):
        return lax.rem(self.me + relative + 2 * self.n, self.n)

    def cross(self, relative):
        if self.partner is not None:
            got = self.view(self.block(relative), None)
            self.net.send(got, got, self.cross_send, self.cross_recv, self.partner)

    def arrive(self, relative):
        relative %= self.n
        if relative not in self.here:
            self.here.add(relative)
            self.net.wait(self.view(self.block(relative), None), self.recv[relative])
            return relative
        return None

    def start(self):
        if self.pieces is not None:
            self.pieces(0, self.home_sem, self.recv[0])
        self.stage(0)
        if self.pieces is None:
            self.cross(0)

    def stage(self, i):
        for want, half, o in self.stages[i]:
            if self.pieces is not None and want == 0 and i == 0:
                self.pieces(o, self.sem, self.recv[-o % self.n])
                continue
            new = self.arrive(want)
            got = self.view(self.block(want), half)
            self.net.send(got, got, self.sem, self.recv[(want - o) % self.n], self.device(o))
            if new is not None:
                self.cross(new)

    def finish(self):
        for relative in self.recv:
            new = self.arrive(relative)
            if new is not None:
                self.cross(new)

    def finish_cross(self):
        self.net.wait(self.other, self.cross_recv)


def interleave(*gathers):
    for i in range(1, max(len(g.stages) for g in gathers)):
        for g in gathers:
            if i < len(g.stages):
                g.stage(i)


def spread(pattern, rows):
    lane = lax.broadcasted_iota(jnp.int32, (rows // 2, 256), 1)
    halves = []
    for i in range(2):
        e = [pattern[i, j].astype(jnp.float32) for j in range(4)]
        low = jnp.where(lane < 64, e[0], e[1])
        high = jnp.where(lane < 192, e[2], e[3])
        halves.append(jnp.where(lane < 128, low, high))
    return jnp.concatenate(halves, axis=0)


def kernel(
    ny, nz, den_hbm, cot_hbm, pat_hbm, fil_hbm, pur_ref, grad_ref, den_ref, cot_ref, pat_ref, fil_ref,
    am, aw, asq, ag, bm, bw, bg, keep_mine, keep_tile, part_s, part_g, wire_s, wire_g, got_s, got_g, square_end,
    total, end_p, end_g, got_p, got_d, sems,
):
    row, col = lax.axis_index("row"), lax.axis_index("col")
    x, y = lax.rem(row, X), lax.div(row, X)
    core, z = lax.rem(col, 2), lax.div(col, 2)
    slot, home = lax.rem(x, 2), lax.div(x, 2)

    def dev(yy, xx, zz, cc):
        return (yy * X + xx, zz * 2 + cc)

    def along_y(o, xx, cc):
        return dev(lax.rem(y + o + ny, ny), xx, z, cc)

    def along_z(o, xx, cc):
        return dev(y, xx, lax.rem(z + o + nz, nz), cc)

    def at_y(o):
        return along_y(o, x, core)

    def at_z(o):
        return along_z(o, x, core)

    partner = dev(y, x, z, 1 - core)
    others = [partner]
    for d in range(1, X):
        there = lax.rem(x + d, X)
        others += [dev(y, there, z, core), dev(y, there, z, 1 - core)]
    for n, along in ((ny, along_y), (nz, along_z)):
        for o in OFFSETS if n == 8 else range(1, n):
            others += [along(o, x, core)]
            if abs(o) == 2 or n != 8:
                others += [along(o, 2 * core, home), along(o, 2 * core + 1, home)]

    barrier = pltpu.get_barrier_semaphore()
    for other in others:
        pl.semaphore_signal(barrier, inc=1, device_id=other, device_id_type=MESH)
    loads = ((den_hbm, den_ref), (cot_hbm, cot_ref), (pat_hbm, pat_ref), (fil_hbm, fil_ref))
    loads = [pltpu.make_async_copy(src, dst, sems.at[N_SEM + i]) for i, (src, dst) in enumerate(loads)]
    for load in loads:
        load.start()
    for load in loads:
        load.wait()
    keep_p = spread(pat_ref, 128)
    keep_f = spread(fil_ref, 128)
    bm[y, core] = (den_ref[...].astype(jnp.float32) * keep_p).astype(jnp.bfloat16)
    bw[y, core] = (-2.0 * cot_ref[...].astype(jnp.float32) * keep_f).astype(jnp.bfloat16)
    keep_mine[...] = keep_f.astype(jnp.bfloat16)
    pl.semaphore_wait(barrier, len(others))

    net = Net(sems, am, home == core)

    def swap_pieces(src, dst, along):
        def pieces(o, send, recv):
            for j in range(2):
                there = along(o, 2 * core + j, home)
                if o == 0:
                    is_self = jnp.logical_and(x == 2 * core + j, home == core)
                    net.send_or_keep(src(j), dst(slot), send, recv, there, is_self)
                else:
                    net.send(src(j), dst(slot), send, recv, there)

        return pieces

    def swap(src, dst):
        send, recv = net.take(), net.take()
        swap_pieces(src, dst, along_z)(0, send, recv)
        net.sent(send, 2, 1)
        return recv

    def to_rows(own, tile):
        return (lambda j: own.at[:, pl.ds(128 * j, 128)]), (lambda s: tile.at[pl.ds(pl.multiple_of(128 * s, 128), 128), :])

    def to_cols(tile, own):
        return (lambda j: tile.at[pl.ds(128 * j, 128), :]), (lambda s: own.at[:, pl.ds(pl.multiple_of(128 * s, 128), 128)])

    def rows_half(ref, half, size):
        return ref if half is None else ref.at[pl.ds(half * size, size), :]

    def b_gather(buf, plan, pieces=None):
        return Gather(
            net, lambda k, h: rows_half(buf.at[k, core], h, 64), y, ny, at_y, plan, pieces, partner, buf.at[:, 1 - core]
        )

    def a_gather(buf, plan, pieces=None):
        return Gather(net, lambda k, h: rows_half(buf.at[k], h, 128), z, nz, at_z, plan, pieces)

    def product(a, b, h):
        left = jnp.concatenate([a[k] for k in range(nz)], axis=1)
        right = b[:, h].reshape(ny * 128, 256)
        return jnp.dot(left, right, preferred_element_type=jnp.float32)

    def part(a, b, to, wire):
        for h in range(2):
            value = product(a, b, h)
            for i in range(2):
                to[2 * h + i] = value[:, 128 * i : 128 * i + 128]
                wire[2 * h + i] = value[:, 128 * i : 128 * i + 128].astype(MID_TYPE)

    def reduce_start(src, dst):
        send, recv = net.take(), net.take()
        for d in (2, 1, 3):
            there = lax.rem(x + d, X)
            net.send(src.at[there], dst.at[d], send, recv, dev(y, there, z, core))
        net.sent(send, 6 if MID_TYPE == jnp.bfloat16 else 12)
        return recv

    def reduce_end(src, dst, recv):
        net.wait(dst.at[pl.ds(1, X - 1)], recv)
        total = src[x]
        for d in range(1, X):
            total = total + dst[d].astype(jnp.float32)
        return total

    def end_start(src, dst):
        send, recv = net.take(), net.take()
        for j in range(2):
            for h in range(2):
                is_self = jnp.logical_and(x == 2 * core + j, core == h)
                net.send_or_keep(src.at[j, h], dst.at[x], send, recv, dev(y, 2 * core + j, z, h), is_self)
        scale = 1 if END_TYPE == jnp.bfloat16 else 2
        net.sent(send, 8 * scale, 6 * scale)
        return recv

    def end_sum(dst, recv):
        net.wait(dst, recv)
        value = dst[0].astype(jnp.float32)
        for s in range(1, X):
            value = value + dst[s].astype(jnp.float32)
        return value

    def split(value, h, to):
        for j in range(2):
            to[j, h] = value[128 * j : 128 * j + 128].astype(END_TYPE)

    w_src, w_dst = to_rows(bw.at[y, core], aw.at[z])
    m_src, m_dst = to_rows(bm.at[y, core], am.at[z])
    f_src, f_dst = to_rows(keep_mine, keep_tile)
    all_bm = b_gather(bm, PLAN["bm"])
    all_bw = b_gather(bw, PLAN["bw"])
    all_aw = a_gather(aw, PLAN["aw"], swap_pieces(w_src, w_dst, along_z))
    all_am = a_gather(am, PLAN["am"], swap_pieces(m_src, m_dst, along_z))
    all_aw.start()
    all_bm.start()
    all_am.start()
    f_recv = swap(f_src, f_dst)
    interleave(all_bm, all_aw, all_am)
    all_bm.finish()
    all_aw.finish()
    all_bm.finish_cross()

    part(aw, bm, part_g, wire_g)
    g_recv = reduce_start(wire_g, got_g)
    all_am.finish()
    part(am, bm, part_s, wire_s)
    s_recv = reduce_start(wire_s, got_s)
    all_bw.start()
    net.wait(keep_tile, f_recv)

    grad = -1.5 * aw[z].astype(jnp.float32) + reduce_end(part_g, got_g, g_recv)
    ag[z] = (grad * keep_tile[...].astype(jnp.float32)).astype(jnp.bfloat16)
    all_ag = a_gather(ag, PLAN["ag"])
    g_src = to_cols(ag.at[z], None)[0]
    g_dst = lambda s: bg.at[y, home, :, pl.ds(pl.multiple_of(128 * s, 128), 128)]
    g_pieces = swap_pieces(g_src, g_dst, along_y)
    all_bg = b_gather(bg, PLAN["bg"], g_pieces)
    all_bg.start()
    all_ag.start()

    asq[z] = (reduce_end(part_s, got_s, s_recv) * keep_tile[...].astype(jnp.float32)).astype(jnp.bfloat16)
    all_as = a_gather(asq, PLAN["asq"])
    all_as.start()
    interleave(all_bw)
    q_src, q_dst = to_cols(asq.at[z], square_end)
    q_recv = swap(q_src, q_dst)
    interleave(all_ag, all_bg, all_as)
    all_bw.finish()
    all_as.finish()
    all_bw.finish_cross()

    for h in range(2):
        split(product(asq, bm, h), h, end_p)
    p_recv = end_start(end_p, got_p)
    for h in range(2):
        total[h] = product(asq, bw, h)
    all_ag.finish()
    for h in range(2):
        total[h] += product(ag, bm, h)
    all_bg.finish()
    split(total[core] + product(am, bg, core), core, end_g)
    all_bg.finish_cross()
    split(total[1 - core] + product(am, bg, 1 - core), 1 - core, end_g)
    d_recv = end_start(end_g, got_d)

    net.wait(square_end, q_recv)
    cubic = end_sum(got_p, p_recv) * keep_mine[...].astype(jnp.float32)
    pur_ref[...] = (3.0 * square_end[...].astype(jnp.float32) - 2.0 * cubic).astype(jnp.bfloat16)
    grad_ref[...] = (end_sum(got_d, d_recv) * spread(pat_ref, 128)).astype(jnp.bfloat16)
    net.drain()


def on_device(ny, nz, density, cotangent, block_pattern, filter_pattern):
    bf16, f32 = jnp.bfloat16, jnp.float32
    left = pltpu.VMEM((nz, 256, 128), bf16)
    right = pltpu.VMEM((ny, 2, 128, 256), bf16)
    block = pltpu.VMEM((128, 256), bf16)
    vmem = pl.BlockSpec(memory_space=pltpu.VMEM)
    return pl.pallas_call(
        functools.partial(kernel, ny, nz),
        out_shape=(jax.ShapeDtypeStruct((128, 256), bf16),) * 2,
        in_specs=[pl.BlockSpec(memory_space=pl.ANY)] * 4,
        out_specs=(vmem, vmem),
        scratch_shapes=[block] * 2
        + [pltpu.SMEM((2, 4), jnp.int32)] * 2
        + [left] * 4
        + [right] * 3
        + [
            block,
            pltpu.VMEM((256, 128), bf16),
            pltpu.VMEM((X, 256, 128), f32),
            pltpu.VMEM((X, 256, 128), f32),
            pltpu.VMEM((X, 256, 128), MID_TYPE),
            pltpu.VMEM((X, 256, 128), MID_TYPE),
            pltpu.VMEM((X, 256, 128), MID_TYPE),
            pltpu.VMEM((X, 256, 128), MID_TYPE),
            block,
            pltpu.VMEM((2, 256, 256), f32),
            pltpu.VMEM((2, 2, 128, 256), END_TYPE),
            pltpu.VMEM((2, 2, 128, 256), END_TYPE),
            pltpu.VMEM((X, 128, 256), END_TYPE),
            pltpu.VMEM((X, 128, 256), END_TYPE),
            pltpu.SemaphoreType.DMA((N_SEM + 4,)),
        ],
        compiler_params=pltpu.CompilerParams(collective_id=0, has_side_effects=True),
    )(density, cotangent, block_pattern, filter_pattern)


def solution(mesh):
    ny, nz = mesh.shape["row"] // X, mesh.shape["col"] // 2
    placed = (P("row", "col"),) * 4
    return jax.shard_map(
        functools.partial(on_device, ny, nz),
        mesh=mesh,
        in_specs=placed,
        out_specs=(P("row", "col"), P("row", "col")),
        check_vma=False,
    )
```
